32 devices in a mesh: field: 4 (over z), vrow: 2 (over core), vcol: 4 (over y, x).
Axes of the slice: x: 2, y: 2, z: 4, core: 2. Of those that a mesh axis runs over, the one named last changes fastest.
Arguments:
- blocks: bfloat16 [1024, 24, 2, 256], P(('vrow', 'vcol'), 'field'), may hold values from 0 to 1
- block_ids: int32 [8, 4, 6], P(('vrow', 'vcol'), 'field'), may hold values from 0 to 11, as said below
- block_counts: int32 [8, 4], P(('vrow', 'vcol'), 'field'), may hold values from 1 to 6, as said below
Outputs:
- tables: float32 [1024, 2, 2, 4, 2, 128], P(('vrow', 'field'), None, None, 'vcol')
The draws below stay inside these ranges and needn't reach their ends.
Inputs may be any that keep to these rules, and one draw needn't show every extreme that they name: `block_ids`: within each row of the last dimension the entries are distinct. `block_counts`: 6 is reached in every draw.
All inputs are finite; a program needn't handle non-finite values.
Results may differ from the reference program's by a relative error of at most 0.0003.
Values may be sent and summed in bfloat16 or wider, within the bound.
A program may use at most 64 MiB of HBM per device.

```python
import jax
import jax.numpy as jnp
from jax import lax

VS = 128
SBLK = 12
BLOCK = 256
OCC = 6
NSH = 8
V = 1024
NSAMP = 12288
N_FIELD = 4
N_VROW = 2
N_VCOL = 4


def draw_block_ids(key, part):
    keys = jax.random.split(jax.random.fold_in(key, 11), NSH * N_FIELD)
    picks = jax.vmap(lambda k: jax.random.permutation(k, SBLK)[:OCC])(keys)
    return picks.reshape(NSH, N_FIELD, OCC).astype(jnp.int32)


def draw_block_counts(key, part):
    first = jax.random.fold_in(key, 23)
    values = jax.random.randint(first, (NSH * N_FIELD,), 1, OCC + 1)
    where = jax.random.randint(jax.random.fold_in(key, 29), (), 0, NSH * N_FIELD)
    values = values.at[where].set(OCC)
    return values.reshape(NSH, N_FIELD).astype(jnp.int32)


def block_levels(own_key, dims, shards, smallest, top_value):
    def one(axis_at, parts):
        heights = jax.random.uniform(jax.random.fold_in(jax.random.fold_in(own_key, 6), axis_at), (parts,), jnp.float32, smallest / len(shards), top_value / len(shards))
        return jnp.repeat(jnp.exp(heights), dims[axis_at] // parts).reshape((-1,) + (1,) * (len(dims) - axis_at - 1))

    gain = one(*shards[0])
    for cut in shards[1:]:
        gain = gain * one(*cut)
    return gain


def setup_inputs(seed: int = 0) -> dict:
    key_of = jax.random.split(jax.random.key(seed), 4)
    return {
        "blocks": jnp.clip(1.0 * jax.random.uniform(key_of[0], (V, N_FIELD * OCC, 2, BLOCK), jnp.float32) ** block_levels(key_of[0], (V, N_FIELD * OCC, 2, BLOCK), ((0, 8), (1, 4)), -0.2, 0.2), 0.0, 1.0).astype(jnp.bfloat16),
        "block_ids": draw_block_ids(jax.random.fold_in(key_of[3], 71), 0),
        "block_counts": draw_block_counts(jax.random.fold_in(key_of[3], 71), 0),
    }


def reference(blocks, block_ids, block_counts):
    occ = block_ids.shape[-1]
    shaped = blocks.reshape(NSH, VS, N_FIELD, occ, 2, BLOCK).astype(jnp.float32)
    slots = jnp.arange(occ, dtype=jnp.int32)
    live = slots[None, None, :] < block_counts[:, :, None]
    onehot = (block_ids[:, :, :, None] == jnp.arange(SBLK, dtype=jnp.int32)[None, None, None, :]) & live[..., None]
    dense = jnp.einsum('sfok,svfocx->svcfkx', onehot.astype(jnp.float32), shaped, precision=lax.Precision.HIGHEST)
    dense = dense.astype(jnp.bfloat16).reshape(NSH * VS * 2, N_FIELD * SBLK * BLOCK).astype(jnp.float32)
    prods = jnp.dot(dense, dense.T, precision=lax.Precision.HIGHEST)
    prods = prods / NSAMP
    prods = prods.reshape(NSH * VS, 2, N_VROW, N_VCOL, VS, 2)
    return jnp.transpose(prods, (0, 1, 2, 3, 5, 4))
```

```python
import functools

import jax
import jax.numpy as jnp
from jax import lax
from jax.experimental import pallas as pl
from jax.experimental.pallas import tpu as pltpu
from jax.sharding import PartitionSpec as P

SBLK = 12
BLOCK = 256
MAX_PIECES = 4
MESH = pl.DeviceIdType.MESH


def partner(q, d, n):
    if n == 4:
        return (q + 1 - 2 * lax.rem(q, 2), lax.rem(q + 2, 4), 3 - q)[d - 1]
    return lax.rem(q + d, n)


def kernel(
    dims, scale, data, meta, out, rows, cols, part, got, rmeta, cmeta, rids, cids,
    col_local, row_local, meta_local,
    row_send, row_recv, col_send, col_recv, rm_send, rm_recv, cm_send, cm_recv,
    part_send, part_recv,
):
    n_field, n_vrow, n_vcol, pieces, occ, width, per_chunk = dims
    f, r, q = lax.axis_index("field"), lax.axis_index("vrow"), lax.axis_index("vcol")
    relay = n_vcol == 4

    barrier = pltpu.get_barrier_semaphore()
    for d in range(1, n_vcol):
        pl.semaphore_signal(barrier, inc=1, device_id={"vcol": partner(q, d, n_vcol)}, device_id_type=MESH)
    for d in range(1, n_vrow):
        pl.semaphore_signal(barrier, inc=1, device_id={"vrow": lax.rem(r + d, n_vrow)}, device_id_type=MESH)
    for d in range(1, n_field):
        pl.semaphore_signal(barrier, inc=1, device_id={"field": lax.rem(f + d, n_field)}, device_id_type=MESH)

    local = []
    for p in range(pieces):
        own = pltpu.make_async_copy(
            data.at[p], cols.at[0, pl.ds(0, occ), :, pl.ds(p * width, width), :], col_local.at[p]
        )
        own.start()
        local.append(own)
        own = pltpu.make_async_copy(data.at[p], rows.at[0, p], row_local.at[p])
        own.start()
        local.append(own)
    own_r = pltpu.make_async_copy(meta, rids.at[0], meta_local.at[0])
    own_r.start()
    own_c = pltpu.make_async_copy(meta, cids.at[0], meta_local.at[1])
    own_c.start()
    for v in range(n_vrow):
        cols[v, occ] = jnp.zeros_like(cols[v, occ])

    pl.semaphore_wait(barrier, n_vcol + n_vrow + n_field - 3)

    sends = []

    def send(src, dst, s, w, where):
        c = pltpu.make_async_remote_copy(
            src_ref=src, dst_ref=dst, send_sem=s, recv_sem=w, device_id=where, device_id_type=MESH
        )
        c.start()
        sends.append(c)
        return c

    row_meta, col_meta, row_copy, col_copy = {}, {}, {}, {}
    for d in range(1, n_vrow):
        to = {"vrow": lax.rem(r + d, n_vrow)}
        col_meta[d] = send(meta, cmeta.at[d], cm_send.at[d], cm_recv.at[d], to)
    for d in range(1, n_vcol):
        to = {"vcol": partner(q, d, n_vcol)}
        row_meta[d] = send(meta, rmeta.at[d], rm_send.at[d], rm_recv.at[d], to)
    for p in range(pieces):
        for d in range(1, n_vrow):
            to = {"vrow": lax.rem(r + d, n_vrow)}
            col_copy[d, p] = send(
                data.at[p],
                cols.at[d, pl.ds(0, occ), :, pl.ds(p * width, width), :],
                col_send.at[d, p], col_recv.at[d, p], to,
            )
        for d in range(1, 3 if relay else n_vcol):
            to = {"vcol": partner(q, d, n_vcol)}
            row_copy[d, p] = send(data.at[p], rows.at[d, p], row_send.at[d, p], row_recv.at[d, p], to)

    for c in local:
        c.wait()
    own_r.wait()
    own_c.wait()
    for d in range(1, n_vrow):
        col_meta[d].wait_recv()
        c = pltpu.make_async_copy(cmeta.at[d], cids.at[d], meta_local.at[1])
        c.start()
        c.wait()
    for d in range(1, n_vrow):
        for p in range(pieces):
            col_copy[d, p].wait_recv()

    half = occ // 2
    match = {}
    part_sends = []

    def matches(d):
        if d:
            row_meta[d].wait_recv()
            c = pltpu.make_async_copy(rmeta.at[d], rids.at[d], meta_local.at[0])
            c.start()
            c.wait()
        theirs = [[cids[v, 0, o] for o in range(occ)] for v in range(n_vrow)]
        found = []
        for o in range(occ):
            mine = rids[d, 0, o]
            for v in range(n_vrow):
                m = jnp.int32(occ)
                for k in range(occ):
                    m = jnp.where((mine >= 0) & (mine == theirs[v][k]), jnp.int32(k), m)
                found.append(m)
        return found

    def compute(d, p):
        if d not in match:
            match[d] = matches(d)
        for v in range(n_vrow):
            acc = None
            for o in range(occ):
                lhs = rows[d, p, o].reshape(2 * width, rows.shape[-1])
                rhs = cols[v, match[d][o * n_vrow + v]]
                rhs = rhs.reshape(rhs.shape[0] * rhs.shape[1], rhs.shape[2])
                t = lax.dot_general(lhs, rhs, (((1,), (1,)), ((), ())), preferred_element_type=jnp.float32)
                acc = t if acc is None else acc + t
            n = acc.shape[1]
            part[d, p, :, v * n : (v + 1) * n] = acc * scale
        s = q if d == 0 else partner(q, d, n_vcol)
        g = s * pieces + p
        dest = g // per_chunk
        place = g - dest * per_chunk
        c = pltpu.make_async_remote_copy(
            src_ref=part.at[d, p],
            dst_ref=got.at[f, place],
            send_sem=part_send.at[d, p],
            recv_sem=part_recv.at[f, place],
            device_id={"field": dest},
            device_id_type=MESH,
        )

        @pl.when(dest != f)
        def _():
            c.start()

        @pl.when(dest == f)
        def _():
            got[f, place] = part[d, p]

        part_sends.append((dest, c))

    for p in range(pieces):
        if relay:
            for p2 in (p,):
                row_copy[1, p2].wait_recv()
                to_y, to_x = {"vcol": partner(q, 2, 4)}, {"vcol": partner(q, 1, 4)}
                a = send(rows.at[1, p2, pl.ds(0, half)], rows.at[3, p2, pl.ds(0, half)],
                         row_send.at[3, p2], row_recv.at[3, p2], to_y)
                row_copy[2, p2].wait_recv()
                b = send(rows.at[2, p2, pl.ds(half, occ - half)], rows.at[3, p2, pl.ds(half, occ - half)],
                         row_send.at[0, p2], row_recv.at[0, p2], to_x)
                row_copy[3, p2] = (a, b)
        compute(0, p)
        if not relay:
            for d in range(1, n_vcol):
                row_copy[d, p].wait_recv()
                compute(d, p)
            continue
        compute(1, p)
        compute(2, p)
        if p:
            for c in row_copy[3, p - 1]:
                c.wait_recv()
            compute(3, p - 1)
    if relay:
        for c in row_copy[3, pieces - 1]:
            c.wait_recv()
        compute(3, pieces - 1)

    for place in range(per_chunk):
        for d in range(1, n_field):
            src = lax.rem(f + d, n_field)
            pltpu.make_async_remote_copy(
                src_ref=part.at[0, 0],
                dst_ref=got.at[src, place],
                send_sem=part_send.at[0, 0],
                recv_sem=part_recv.at[src, place],
                device_id={"field": src},
                device_id_type=MESH,
            ).wait_recv()
        total = got[0, place]
        for k in range(1, n_field):
            total = total + got[k, place]
        out[place] = total
    for c in sends:
        c.wait_send()
    for dest, c in part_sends:
        @pl.when(dest != f)
        def _():
            c.wait_send()


def on_device(blocks, block_ids, block_counts):
    n_field, n_vrow, n_vcol = (lax.axis_size(a) for a in ("field", "vrow", "vcol"))
    vs, occ, ch, x = blocks.shape
    chunk = n_vcol * vs // n_field
    width = min(vs // MAX_PIECES, chunk)
    pieces = vs // width
    per_chunk = chunk // width
    data = blocks.reshape(pieces, width, occ, ch, x).transpose(0, 2, 3, 1, 4)
    slots = jnp.arange(occ, dtype=jnp.int32)
    ids = jnp.where(slots < block_counts[0, 0], block_ids[0, 0], -1)
    meta = jnp.pad(ids[None, :], ((0, 0), (0, 128 - occ)))
    c = ch * vs
    wide = n_vrow * c
    dims = (n_field, n_vrow, n_vcol, pieces, occ, width, per_chunk)
    dma = pltpu.SemaphoreType.DMA
    scale = 1.0 / (n_field * SBLK * BLOCK)
    out = pl.pallas_call(
        functools.partial(kernel, dims, scale),
        out_shape=jax.ShapeDtypeStruct((per_chunk, ch * width, wide), jnp.float32),
        in_specs=[pl.BlockSpec(memory_space=pl.ANY), pl.BlockSpec(memory_space=pltpu.VMEM)],
        out_specs=pl.BlockSpec(memory_space=pltpu.VMEM),
        scratch_shapes=[
            pltpu.VMEM((n_vcol, pieces, occ, ch, width, x), jnp.bfloat16),
            pltpu.VMEM((n_vrow, occ + 1, ch, vs, x), jnp.bfloat16),
            pltpu.VMEM((n_vcol, pieces, ch * width, wide), jnp.float32),
            pltpu.VMEM((n_field, per_chunk, ch * width, wide), jnp.float32),
            pltpu.VMEM((n_vcol, 1, 128), jnp.int32),
            pltpu.VMEM((n_vrow, 1, 128), jnp.int32),
            pltpu.SMEM((n_vcol, 1, 128), jnp.int32),
            pltpu.SMEM((n_vrow, 1, 128), jnp.int32),
            dma((pieces,)),
            dma((pieces,)),
            dma((2,)),
            dma((n_vcol, pieces)),
            dma((n_vcol, pieces)),
            dma((n_vrow, pieces)),
            dma((n_vrow, pieces)),
            dma((n_vcol,)),
            dma((n_vcol,)),
            dma((n_vrow,)),
            dma((n_vrow,)),
            dma((n_vcol, pieces)),
            dma((n_field, per_chunk)),
        ],
        compiler_params=pltpu.CompilerParams(collective_id=0, has_side_effects=True),
    )(data, meta)
    out = out.reshape(per_chunk, ch, width, n_vrow, ch, vs)
    r = lax.axis_index("vrow")
    turned = jnp.concatenate([out[:, :, :, k:k+1] for k in range(n_vrow)] , axis=3) if n_vrow == 1 else (
        jnp.where(r == 0, out, jnp.roll(out, 1, axis=3)) if n_vrow == 2 else jnp.roll(out, r, axis=3)
    )
    return turned.transpose(0, 2, 1, 3, 4, 5).reshape(chunk, ch, n_vrow, 1, ch, vs)


def solution(mesh):
    placed = (
        P(("vrow", "vcol"), "field", None, None),
        P(("vrow", "vcol"), "field", None),
        P(("vrow", "vcol"), "field"),
    )
    return jax.shard_map(
        on_device,
        mesh=mesh,
        in_specs=placed,
        out_specs=P(("vrow", "field"), None, None, "vcol", None, None),
        check_vma=False,
    )
```

```python
import functools

import jax
import jax.numpy as jnp
from jax import lax
from jax.experimental import pallas as pl
from jax.experimental.pallas import tpu as pltpu
from jax.sharding import PartitionSpec as P

SBLK = 12
BLOCK = 256
MAX_PIECES = 4
LEVELS = 65535.0
HALF = 32768
MESH = pl.DeviceIdType.MESH


def partner(q, d, n):
    if n == 4:
        return (q + 1 - 2 * lax.rem(q, 2), lax.rem(q + 2, 4), 3 - q)[d - 1]
    return lax.rem(q + d, n)


def kernel(
    dims, scale, data, meta, out, rows, cols, part, code, tops, got, got_tops, mine_sum, rmeta, cmeta, rids, cids,
    col_local, row_local, meta_local,
    row_send, row_recv, col_send, col_recv, rm_send, rm_recv, cm_send, cm_recv,
    part_send, part_recv, top_send, top_recv,
):
    n_field, n_vrow, n_vcol, pieces, occ, width, per_chunk = dims
    f, r, q = lax.axis_index("field"), lax.axis_index("vrow"), lax.axis_index("vcol")
    relay = n_vcol == 4

    barrier = pltpu.get_barrier_semaphore()
    for d in range(1, n_vcol):
        pl.semaphore_signal(barrier, inc=1, device_id={"vcol": partner(q, d, n_vcol)}, device_id_type=MESH)
    for d in range(1, n_vrow):
        pl.semaphore_signal(barrier, inc=1, device_id={"vrow": lax.rem(r + d, n_vrow)}, device_id_type=MESH)
    for d in range(1, n_field):
        pl.semaphore_signal(barrier, inc=1, device_id={"field": lax.rem(f + d, n_field)}, device_id_type=MESH)

    local = []
    for p in range(pieces):
        own = pltpu.make_async_copy(
            data.at[p], cols.at[0, pl.ds(0, occ), :, pl.ds(p * width, width), :], col_local.at[p]
        )
        own.start()
        local.append(own)
        own = pltpu.make_async_copy(data.at[p], rows.at[0, p], row_local.at[p])
        own.start()
        local.append(own)
    own_r = pltpu.make_async_copy(meta, rids.at[0], meta_local.at[0])
    own_r.start()
    own_c = pltpu.make_async_copy(meta, cids.at[0], meta_local.at[1])
    own_c.start()
    for v in range(n_vrow):
        cols[v, occ] = jnp.zeros_like(cols[v, occ])

    pl.semaphore_wait(barrier, n_vcol + n_vrow + n_field - 3)

    sends = []

    def send(src, dst, s, w, where):
        c = pltpu.make_async_remote_copy(
            src_ref=src, dst_ref=dst, send_sem=s, recv_sem=w, device_id=where, device_id_type=MESH
        )
        c.start()
        sends.append(c)
        return c

    row_meta, col_meta, row_copy, col_copy = {}, {}, {}, {}
    for d in range(1, n_vrow):
        to = {"vrow": lax.rem(r + d, n_vrow)}
        col_meta[d] = send(meta, cmeta.at[d], cm_send.at[d], cm_recv.at[d], to)
    for d in range(1, n_vcol):
        to = {"vcol": partner(q, d, n_vcol)}
        row_meta[d] = send(meta, rmeta.at[d], rm_send.at[d], rm_recv.at[d], to)
    for p in range(pieces):
        for d in range(1, n_vrow):
            to = {"vrow": lax.rem(r + d, n_vrow)}
            col_copy[d, p] = send(
                data.at[p],
                cols.at[d, pl.ds(0, occ), :, pl.ds(p * width, width), :],
                col_send.at[d, p], col_recv.at[d, p], to,
            )
        for d in range(1, 3 if relay else n_vcol):
            to = {"vcol": partner(q, d, n_vcol)}
            row_copy[d, p] = send(data.at[p], rows.at[d, p], row_send.at[d, p], row_recv.at[d, p], to)

    for c in local:
        c.wait()
    own_r.wait()
    own_c.wait()
    for d in range(1, n_vrow):
        col_meta[d].wait_recv()
        c = pltpu.make_async_copy(cmeta.at[d], cids.at[d], meta_local.at[1])
        c.start()
        c.wait()
    for d in range(1, n_vrow):
        for p in range(pieces):
            col_copy[d, p].wait_recv()

    half = occ // 2
    match = {}
    part_sends = []

    def matches(d):
        if d:
            row_meta[d].wait_recv()
            c = pltpu.make_async_copy(rmeta.at[d], rids.at[d], meta_local.at[0])
            c.start()
            c.wait()
        theirs = [[cids[v, 0, o] for o in range(occ)] for v in range(n_vrow)]
        found = []
        for o in range(occ):
            mine = rids[d, 0, o]
            for v in range(n_vrow):
                m = jnp.int32(occ)
                for k in range(occ):
                    m = jnp.where((mine >= 0) & (mine == theirs[v][k]), jnp.int32(k), m)
                found.append(m)
        return found

    def compute(d, p):
        if d not in match:
            match[d] = matches(d)
        for v in range(n_vrow):
            acc = None
            for o in range(occ):
                lhs = rows[d, p, o].reshape(2 * width, rows.shape[-1])
                rhs = cols[v, match[d][o * n_vrow + v]]
                rhs = rhs.reshape(rhs.shape[0] * rhs.shape[1], rhs.shape[2])
                t = lax.dot_general(lhs, rhs, (((1,), (1,)), ((), ())), preferred_element_type=jnp.float32)
                acc = t if acc is None else acc + t
            n = acc.shape[1]
            at = pl.multiple_of(lax.rem(r + v, n_vrow) * n, n)
            part[d, p, :, pl.ds(at, n)] = acc
            top = jnp.max(acc, axis=0, keepdims=True)
            inverse = jnp.where(top > 0, 1.0 / top, 0.0)
            level = ((acc * inverse) * LEVELS + 0.5).astype(jnp.int32) - HALF
            code[d, p, :, pl.ds(at, n)] = level.astype(jnp.int16)
            tops[d, p, :, pl.ds(at, n)] = top
        s = q if d == 0 else partner(q, d, n_vcol)
        g = s * pieces + p
        dest = g // per_chunk
        place = g - dest * per_chunk
        to = {"field": dest}
        c = pltpu.make_async_remote_copy(
            src_ref=code.at[d, p], dst_ref=got.at[f, place],
            send_sem=part_send.at[d, p], recv_sem=part_recv.at[f, place],
            device_id=to, device_id_type=MESH,
        )
        t = pltpu.make_async_remote_copy(
            src_ref=tops.at[d, p], dst_ref=got_tops.at[f, place],
            send_sem=top_send.at[d, p], recv_sem=top_recv.at[f, place],
            device_id=to, device_id_type=MESH,
        )

        @pl.when(dest != f)
        def _():
            t.start()
            c.start()

        @pl.when(dest == f)
        def _():
            mine_sum[place] = part[d, p]

        part_sends.append((dest, c, t))

    def forward(p):
        row_copy[1, p].wait_recv()
        a = send(rows.at[1, p, pl.ds(0, half)], rows.at[3, p, pl.ds(0, half)],
                 row_send.at[3, p], row_recv.at[3, p], {"vcol": partner(q, 2, 4)})
        row_copy[2, p].wait_recv()
        b = send(rows.at[2, p, pl.ds(half, occ - half)], rows.at[3, p, pl.ds(half, occ - half)],
                 row_send.at[0, p], row_recv.at[0, p], {"vcol": partner(q, 1, 4)})
        row_copy[3, p] = (a, b)

    for p in range(pieces):
        compute(0, p)
        if relay:
            forward(p)
        for d in range(1, 3 if relay else n_vcol):
            if not relay:
                row_copy[d, p].wait_recv()
            compute(d, p)
    if relay:
        for p in range(pieces):
            for c in row_copy[3, p]:
                c.wait_recv()
            compute(3, p)

    for place in range(per_chunk):
        total = mine_sum[place]
        for d in range(1, n_field):
            src = lax.rem(f + d, n_field)
            for buf, land, gone, came in (
                (code, got, part_send, part_recv), (tops, got_tops, top_send, top_recv),
            ):
                pltpu.make_async_remote_copy(
                    src_ref=buf.at[0, 0], dst_ref=land.at[src, place],
                    send_sem=gone.at[0, 0], recv_sem=came.at[src, place],
                    device_id={"field": src}, device_id_type=MESH,
                ).wait_recv()
            level = (got[src, place].astype(jnp.int32) + HALF).astype(jnp.float32)
            total = total + level * (got_tops[src, place] * (1.0 / LEVELS))
        total = total * scale
        ch, n_r, ch2, vs = out.shape[1:]
        for a in range(ch):
            for k in range(n_r):
                for b in range(ch2):
                    c0 = (k * ch2 + b) * vs
                    out[pl.ds(place * width, width), a, k, b, :] = total[a * width : (a + 1) * width, c0 : c0 + vs]
    for c in sends:
        c.wait_send()
    for dest, c, t in part_sends:
        @pl.when(dest != f)
        def _():
            c.wait_send()
            t.wait_send()


def on_device(blocks, block_ids, block_counts):
    n_field, n_vrow, n_vcol = (lax.axis_size(a) for a in ("field", "vrow", "vcol"))
    vs, occ, ch, x = blocks.shape
    chunk = n_vcol * vs // n_field
    width = min(vs // MAX_PIECES, chunk)
    pieces = vs // width
    per_chunk = chunk // width
    data = blocks.reshape(pieces, width, occ, ch, x).transpose(0, 2, 3, 1, 4)
    slots = jnp.arange(occ, dtype=jnp.int32)
    ids = jnp.where(slots < block_counts[0, 0], block_ids[0, 0], -1)
    meta = jnp.pad(ids[None, :], ((0, 0), (0, 128 - occ)))
    c = ch * vs
    wide = n_vrow * c
    dims = (n_field, n_vrow, n_vcol, pieces, occ, width, per_chunk)
    dma = pltpu.SemaphoreType.DMA
    scale = 1.0 / (n_field * SBLK * BLOCK)
    out = pl.pallas_call(
        functools.partial(kernel, dims, scale),
        out_shape=jax.ShapeDtypeStruct((chunk, ch, n_vrow, ch, vs), jnp.float32),
        in_specs=[pl.BlockSpec(memory_space=pl.ANY), pl.BlockSpec(memory_space=pltpu.VMEM)],
        out_specs=pl.BlockSpec(memory_space=pltpu.VMEM),
        scratch_shapes=[
            pltpu.VMEM((n_vcol, pieces, occ, ch, width, x), jnp.bfloat16),
            pltpu.VMEM((n_vrow, occ + 1, ch, vs, x), jnp.bfloat16),
            pltpu.VMEM((n_vcol, pieces, ch * width, wide), jnp.float32),
            pltpu.VMEM((n_vcol, pieces, ch * width, wide), jnp.int16),
            pltpu.VMEM((n_vcol, pieces, 1, wide), jnp.float32),
            pltpu.VMEM((n_field, per_chunk, ch * width, wide), jnp.int16),
            pltpu.VMEM((n_field, per_chunk, 1, wide), jnp.float32),
            pltpu.VMEM((per_chunk, ch * width, wide), jnp.float32),
            pltpu.VMEM((n_vcol, 1, 128), jnp.int32),
            pltpu.VMEM((n_vrow, 1, 128), jnp.int32),
            pltpu.SMEM((n_vcol, 1, 128), jnp.int32),
            pltpu.SMEM((n_vrow, 1, 128), jnp.int32),
            dma((pieces,)),
            dma((pieces,)),
            dma((2,)),
            dma((n_vcol, pieces)),
            dma((n_vcol, pieces)),
            dma((n_vrow, pieces)),
            dma((n_vrow, pieces)),
            dma((n_vcol,)),
            dma((n_vcol,)),
            dma((n_vrow,)),
            dma((n_vrow,)),
            dma((n_vcol, pieces)),
            dma((n_field, per_chunk)),
            dma((n_vcol, pieces)),
            dma((n_field, per_chunk)),
        ],
        compiler_params=pltpu.CompilerParams(collective_id=0, has_side_effects=True),
    )(data, meta)
    return out.reshape(chunk, ch, n_vrow, 1, ch, vs)


def solution(mesh):
    placed = (
        P(("vrow", "vcol"), "field", None, None),
        P(("vrow", "vcol"), "field", None),
        P(("vrow", "vcol"), "field"),
    )
    return jax.shard_map(
        on_device,
        mesh=mesh,
        in_specs=placed,
        out_specs=P(("vrow", "field"), None, None, "vcol", None, None),
        check_vma=False,
    )
```

```python
import functools

import jax
import jax.numpy as jnp
from jax import lax
from jax.experimental import pallas as pl
from jax.experimental.pallas import tpu as pltpu
from jax.sharding import PartitionSpec as P

SBLK = 12
BLOCK = 256
MAX_PIECES = 4
AHEAD = 2
LEVELS = 65535.0
HALF = 32768
MESH = pl.DeviceIdType.MESH


def partner(q, d, n):
    if n == 4:
        return (q + 1 - 2 * lax.rem(q, 2), lax.rem(q + 2, 4), 3 - q)[d - 1]
    return lax.rem(q + d, n)


def kernel(
    dims, scale, data, meta, out, rows, cols, part, code, tops, got, got_tops, mine_sum, rmeta, cmeta, rids, cids,
    col_local, row_local, meta_local,
    row_send, row_recv, col_send, col_recv, rm_send, rm_recv, cm_send, cm_recv,
    part_send, part_recv, top_send, top_recv,
):
    n_field, n_vrow, n_vcol, pieces, occ, width, per_chunk = dims
    f, r, q = lax.axis_index("field"), lax.axis_index("vrow"), lax.axis_index("vcol")
    relay = n_vcol == 4

    barrier = pltpu.get_barrier_semaphore()
    for d in range(1, n_vcol):
        pl.semaphore_signal(barrier, inc=1, device_id={"vcol": partner(q, d, n_vcol)}, device_id_type=MESH)
    for d in range(1, n_vrow):
        pl.semaphore_signal(barrier, inc=1, device_id={"vrow": lax.rem(r + d, n_vrow)}, device_id_type=MESH)
    for d in range(1, n_field):
        pl.semaphore_signal(barrier, inc=1, device_id={"field": lax.rem(f + d, n_field)}, device_id_type=MESH)

    local = []
    for p in range(pieces):
        own = pltpu.make_async_copy(
            data.at[p], cols.at[0, pl.ds(0, occ), :, pl.ds(p * width, width), :], col_local.at[p]
        )
        own.start()
        local.append(own)
        own = pltpu.make_async_copy(data.at[p], rows.at[0, p], row_local.at[p])
        own.start()
        local.append(own)
    own_r = pltpu.make_async_copy(meta, rids.at[0], meta_local.at[0])
    own_r.start()
    own_c = pltpu.make_async_copy(meta, cids.at[0], meta_local.at[1])
    own_c.start()
    for v in range(n_vrow):
        cols[v, occ] = jnp.zeros_like(cols[v, occ])

    pl.semaphore_wait(barrier, n_vcol + n_vrow + n_field - 3)

    sends = []

    def send(src, dst, s, w, where):
        c = pltpu.make_async_remote_copy(
            src_ref=src, dst_ref=dst, send_sem=s, recv_sem=w, device_id=where, device_id_type=MESH
        )
        c.start()
        sends.append(c)
        return c

    row_meta, col_meta, row_copy, col_copy = {}, {}, {}, {}

    def send_rows(p):
        for d in range(1, 3 if relay else n_vcol):
            to = {"vcol": partner(q, d, n_vcol)}
            row_copy[d, p] = send(data.at[p], rows.at[d, p], row_send.at[d, p], row_recv.at[d, p], to)

    for d in range(1, n_vrow):
        to = {"vrow": lax.rem(r + d, n_vrow)}
        col_meta[d] = send(meta, cmeta.at[d], cm_send.at[d], cm_recv.at[d], to)
    for d in range(1, n_vcol):
        to = {"vcol": partner(q, d, n_vcol)}
        row_meta[d] = send(meta, rmeta.at[d], rm_send.at[d], rm_recv.at[d], to)
    for p in range(pieces):
        for d in range(1, n_vrow):
            to = {"vrow": lax.rem(r + d, n_vrow)}
            col_copy[d, p] = send(
                data.at[p],
                cols.at[d, pl.ds(0, occ), :, pl.ds(p * width, width), :],
                col_send.at[d, p], col_recv.at[d, p], to,
            )
        if p < (AHEAD if relay else pieces):
            send_rows(p)

    for c in local:
        c.wait()
    own_r.wait()
    own_c.wait()
    for d in range(1, n_vrow):
        col_meta[d].wait_recv()
        c = pltpu.make_async_copy(cmeta.at[d], cids.at[d], meta_local.at[1])
        c.start()
        c.wait()
    for d in range(1, n_vrow):
        for p in range(pieces):
            col_copy[d, p].wait_recv()

    half = occ // 2
    match = {}
    part_sends = []

    def matches(d):
        if d:
            row_meta[d].wait_recv()
            c = pltpu.make_async_copy(rmeta.at[d], rids.at[d], meta_local.at[0])
            c.start()
            c.wait()
        theirs = [[cids[v, 0, o] for o in range(occ)] for v in range(n_vrow)]
        found = []
        for o in range(occ):
            mine = rids[d, 0, o]
            for v in range(n_vrow):
                m = jnp.int32(occ)
                for k in range(occ):
                    m = jnp.where((mine >= 0) & (mine == theirs[v][k]), jnp.int32(k), m)
                found.append(m)
        return found

    def compute(d, p):
        if d not in match:
            match[d] = matches(d)
        for v in range(n_vrow):
            acc = None
            for o in range(occ):
                lhs = rows[d, p, o].reshape(2 * width, rows.shape[-1])
                rhs = cols[v, match[d][o * n_vrow + v]]
                rhs = rhs.reshape(rhs.shape[0] * rhs.shape[1], rhs.shape[2])
                t = lax.dot_general(lhs, rhs, (((1,), (1,)), ((), ())), preferred_element_type=jnp.float32)
                acc = t if acc is None else acc + t
            n = acc.shape[1]
            at = pl.multiple_of(lax.rem(r + v, n_vrow) * n, n)
            part[d, p, :, pl.ds(at, n)] = acc
            top = jnp.max(acc, axis=0, keepdims=True)
            inverse = jnp.where(top > 0, 1.0 / top, 0.0)
            level = ((acc * inverse) * LEVELS + 0.5).astype(jnp.int32) - HALF
            code[d, p, :, pl.ds(at, n)] = level.astype(jnp.int16)
            tops[d, p, :, pl.ds(at, n)] = top
        s = q if d == 0 else partner(q, d, n_vcol)
        g = s * pieces + p
        dest = g // per_chunk
        place = g - dest * per_chunk
        to = {"field": dest}
        c = pltpu.make_async_remote_copy(
            src_ref=code.at[d, p], dst_ref=got.at[f, place],
            send_sem=part_send.at[d, p], recv_sem=part_recv.at[f, place],
            device_id=to, device_id_type=MESH,
        )
        t = pltpu.make_async_remote_copy(
            src_ref=tops.at[d, p], dst_ref=got_tops.at[f, place],
            send_sem=top_send.at[d, p], recv_sem=top_recv.at[f, place],
            device_id=to, device_id_type=MESH,
        )

        @pl.when(dest != f)
        def _():
            t.start()
            c.start()

        @pl.when(dest == f)
        def _():
            mine_sum[place] = part[d, p]

        part_sends.append((dest, c, t))

    def forward(p):
        row_copy[1, p].wait_recv()
        a = send(rows.at[1, p, pl.ds(0, half)], rows.at[3, p, pl.ds(0, half)],
                 row_send.at[3, p], row_recv.at[3, p], {"vcol": partner(q, 2, 4)})
        row_copy[2, p].wait_recv()
        b = send(rows.at[2, p, pl.ds(half, occ - half)], rows.at[3, p, pl.ds(half, occ - half)],
                 row_send.at[0, p], row_recv.at[0, p], {"vcol": partner(q, 1, 4)})
        row_copy[3, p] = (a, b)
        if p + AHEAD < pieces:
            send_rows(p + AHEAD)

    compute(0, 0)
    for p in range(pieces):
        if relay:
            forward(p)
        for d in range(1, 3 if relay else n_vcol):
            if not relay:
                row_copy[d, p].wait_recv()
            compute(d, p)
        if p + 1 < pieces:
            compute(0, p + 1)
        if relay and p:
            for c in row_copy[3, p - 1]:
                c.wait_recv()
            compute(3, p - 1)
    if relay:
        for c in row_copy[3, pieces - 1]:
            c.wait_recv()
        compute(3, pieces - 1)

    for place in range(per_chunk):
        total = mine_sum[place]
        for d in range(1, n_field):
            src = lax.rem(f + d, n_field)
            for buf, land, gone, came in (
                (code, got, part_send, part_recv), (tops, got_tops, top_send, top_recv),
            ):
                pltpu.make_async_remote_copy(
                    src_ref=buf.at[0, 0], dst_ref=land.at[src, place],
                    send_sem=gone.at[0, 0], recv_sem=came.at[src, place],
                    device_id={"field": src}, device_id_type=MESH,
                ).wait_recv()
            level = (got[src, place].astype(jnp.int32) + HALF).astype(jnp.float32)
            total = total + level * (got_tops[src, place] * (1.0 / LEVELS))
        total = total * scale
        ch, n_r, ch2, vs = out.shape[1:]
        for a in range(ch):
            for k in range(n_r):
                for b in range(ch2):
                    c0 = (k * ch2 + b) * vs
                    out[pl.ds(place * width, width), a, k, b, :] = total[a * width : (a + 1) * width, c0 : c0 + vs]
    for c in sends:
        c.wait_send()
    for dest, c, t in part_sends:
        @pl.when(dest != f)
        def _():
            c.wait_send()
            t.wait_send()


def on_device(blocks, block_ids, block_counts):
    n_field, n_vrow, n_vcol = (lax.axis_size(a) for a in ("field", "vrow", "vcol"))
    vs, occ, ch, x = blocks.shape
    chunk = n_vcol * vs // n_field
    width = min(vs // MAX_PIECES, chunk)
    pieces = vs // width
    per_chunk = chunk // width
    data = blocks.reshape(pieces, width, occ, ch, x).transpose(0, 2, 3, 1, 4)
    slots = jnp.arange(occ, dtype=jnp.int32)
    ids = jnp.where(slots < block_counts[0, 0], block_ids[0, 0], -1)
    meta = jnp.pad(ids[None, :], ((0, 0), (0, 128 - occ)))
    c = ch * vs
    wide = n_vrow * c
    dims = (n_field, n_vrow, n_vcol, pieces, occ, width, per_chunk)
    dma = pltpu.SemaphoreType.DMA
    scale = 1.0 / (n_field * SBLK * BLOCK)
    out = pl.pallas_call(
        functools.partial(kernel, dims, scale),
        out_shape=jax.ShapeDtypeStruct((chunk, ch, n_vrow, ch, vs), jnp.float32),
        in_specs=[pl.BlockSpec(memory_space=pl.ANY), pl.BlockSpec(memory_space=pltpu.VMEM)],
        out_specs=pl.BlockSpec(memory_space=pltpu.VMEM),
        scratch_shapes=[
            pltpu.VMEM((n_vcol, pieces, occ, ch, width, x), jnp.bfloat16),
            pltpu.VMEM((n_vrow, occ + 1, ch, vs, x), jnp.bfloat16),
            pltpu.VMEM((n_vcol, pieces, ch * width, wide), jnp.float32),
            pltpu.VMEM((n_vcol, pieces, ch * width, wide), jnp.int16),
            pltpu.VMEM((n_vcol, pieces, 1, wide), jnp.float32),
            pltpu.VMEM((n_field, per_chunk, ch * width, wide), jnp.int16),
            pltpu.VMEM((n_field, per_chunk, 1, wide), jnp.float32),
            pltpu.VMEM((per_chunk, ch * width, wide), jnp.float32),
            pltpu.VMEM((n_vcol, 1, 128), jnp.int32),
            pltpu.VMEM((n_vrow, 1, 128), jnp.int32),
            pltpu.SMEM((n_vcol, 1, 128), jnp.int32),
            pltpu.SMEM((n_vrow, 1, 128), jnp.int32),
            dma((pieces,)),
            dma((pieces,)),
            dma((2,)),
            dma((n_vcol, pieces)),
            dma((n_vcol, pieces)),
            dma((n_vrow, pieces)),
            dma((n_vrow, pieces)),
            dma((n_vcol,)),
            dma((n_vcol,)),
            dma((n_vrow,)),
            dma((n_vrow,)),
            dma((n_vcol, pieces)),
            dma((n_field, per_chunk)),
            dma((n_vcol, pieces)),
            dma((n_field, per_chunk)),
        ],
        compiler_params=pltpu.CompilerParams(collective_id=0, has_side_effects=True),
    )(data, meta)
    return out.reshape(chunk, ch, n_vrow, 1, ch, vs)


def solution(mesh):
    placed = (
        P(("vrow", "vcol"), "field", None, None),
        P(("vrow", "vcol"), "field", None),
        P(("vrow", "vcol"), "field"),
    )
    return jax.shard_map(
        on_device,
        mesh=mesh,
        in_specs=placed,
        out_specs=P(("vrow", "field"), None, None, "vcol", None, None),
        check_vma=False,
    )
```

```python
import functools

import jax
import jax.numpy as jnp
from jax import lax
from jax.experimental import pallas as pl
from jax.experimental.pallas import tpu as pltpu
from jax.sharding import PartitionSpec as P

SBLK = 12
BLOCK = 256
MAX_PIECES = 4
AHEAD = 2
LEVELS = 65535.0
HALF = 32768
MESH = pl.DeviceIdType.MESH


def partner(q, d, n):
    if n == 4:
        return (q + 1 - 2 * lax.rem(q, 2), lax.rem(q + 2, 4), 3 - q)[d - 1]
    return lax.rem(q + d, n)


def kernel(
    dims, scale, data, meta, out, rows, raw_cols, cols, part, code, tops, got, got_tops, mine_sum, rmeta, cmeta, rids, cids,
    row_local, meta_local,
    row_send, row_recv, col_send, col_recv, rm_send, rm_recv, cm_send, cm_recv,
    part_send, part_recv, top_send, top_recv,
):
    n_field, n_vrow, n_vcol, pieces, occ, width, per_chunk = dims
    f, r, q = lax.axis_index("field"), lax.axis_index("vrow"), lax.axis_index("vcol")
    relay = n_vcol == 4

    barrier = pltpu.get_barrier_semaphore()
    for d in range(1, n_vcol):
        pl.semaphore_signal(barrier, inc=1, device_id={"vcol": partner(q, d, n_vcol)}, device_id_type=MESH)
    for d in range(1, n_vrow):
        pl.semaphore_signal(barrier, inc=1, device_id={"vrow": lax.rem(r + d, n_vrow)}, device_id_type=MESH)
    for d in range(1, n_field):
        pl.semaphore_signal(barrier, inc=1, device_id={"field": lax.rem(f + d, n_field)}, device_id_type=MESH)

    own = pltpu.make_async_copy(data, rows.at[0], row_local.at[0])
    own.start()
    own_r = pltpu.make_async_copy(meta, rids.at[0], meta_local.at[0])
    own_r.start()
    own_c = pltpu.make_async_copy(meta, cids.at[0], meta_local.at[1])
    own_c.start()
    for v in range(n_vrow):
        cols[v, occ] = jnp.zeros_like(cols[v, occ])

    pl.semaphore_wait(barrier, n_vcol + n_vrow + n_field - 3)

    def span(p):
        return pl.ds(p * width, width)

    sends = []

    def send(src, dst, s, w, where):
        c = pltpu.make_async_remote_copy(
            src_ref=src, dst_ref=dst, send_sem=s, recv_sem=w, device_id=where, device_id_type=MESH
        )
        c.start()
        sends.append(c)
        return c

    row_meta, col_meta, row_copy, col_copy = {}, {}, {}, {}

    def send_rows(p):
        for d in range(1, 3 if relay else n_vcol):
            to = {"vcol": partner(q, d, n_vcol)}
            row_copy[d, p] = send(data.at[span(p)], rows.at[d, span(p)], row_send.at[d, p], row_recv.at[d, p], to)

    for d in range(1, n_vrow):
        to = {"vrow": lax.rem(r + d, n_vrow)}
        col_meta[d] = send(meta, cmeta.at[d], cm_send.at[d], cm_recv.at[d], to)
    for d in range(1, n_vcol):
        to = {"vcol": partner(q, d, n_vcol)}
        row_meta[d] = send(meta, rmeta.at[d], rm_send.at[d], rm_recv.at[d], to)
    for p in range(pieces):
        for d in range(1, n_vrow):
            to = {"vrow": lax.rem(r + d, n_vrow)}
            col_copy[d, p] = send(
                data.at[span(p)],
                raw_cols.at[d, span(p)],
                col_send.at[d, p], col_recv.at[d, p], to,
            )
        if p < (AHEAD if relay else pieces):
            send_rows(p)

    own.wait()
    own_r.wait()
    own_c.wait()
    for d in range(1, n_vrow):
        col_meta[d].wait_recv()
        c = pltpu.make_async_copy(cmeta.at[d], cids.at[d], meta_local.at[1])
        c.start()
        c.wait()
    for d in range(1, n_vrow):
        for p in range(pieces):
            col_copy[d, p].wait_recv()
    ch, vs = rows.shape[3], rows.shape[1]
    n = ch * vs
    to_row = lax.broadcasted_iota(jnp.int32, (n, n), 0)
    from_row = lax.broadcasted_iota(jnp.int32, (n, n), 1)
    order = jnp.where(from_row == lax.rem(to_row, vs) * ch + to_row // vs, 1.0, 0.0).astype(jnp.bfloat16)
    for v in range(n_vrow):
        for o in range(occ):
            block = (raw_cols[v, :, o] if v else rows[0, :, o]).reshape(n, rows.shape[-1])
            turned = jnp.dot(order, block, preferred_element_type=jnp.float32)
            cols[v, o] = turned.astype(jnp.bfloat16)

    match = {}
    part_sends = []

    def matches(d):
        if d:
            row_meta[d].wait_recv()
            c = pltpu.make_async_copy(rmeta.at[d], rids.at[d], meta_local.at[0])
            c.start()
            c.wait()
        theirs = [[cids[v, 0, o] for o in range(occ)] for v in range(n_vrow)]
        found = []
        for o in range(occ):
            mine = rids[d, 0, o]
            for v in range(n_vrow):
                m = jnp.int32(occ)
                for k in range(occ):
                    m = jnp.where((mine >= 0) & (mine == theirs[v][k]), jnp.int32(k), m)
                found.append(m)
        return found

    def compute(d, p):
        if d not in match:
            match[d] = matches(d)
        for v in range(n_vrow):
            acc = None
            for o in range(occ):
                lhs = rows[d, p * width : (p + 1) * width, o].reshape(ch * width, rows.shape[-1])
                rhs = cols[v, match[d][o * n_vrow + v]]
                t = lax.dot_general(lhs, rhs, (((1,), (1,)), ((), ())), preferred_element_type=jnp.float32)
                acc = t if acc is None else acc + t
            n = acc.shape[1]
            at = pl.multiple_of(lax.rem(r + v, n_vrow) * n, n)
            part[d, p, :, pl.ds(at, n)] = acc
            top = jnp.max(acc, axis=0, keepdims=True)
            inverse = jnp.where(top > 0, 1.0 / top, 0.0)
            level = ((acc * inverse) * LEVELS + 0.5).astype(jnp.int32) - HALF
            code[d, p, :, pl.ds(at, n)] = level.astype(jnp.int16)
            tops[d, p, :, pl.ds(at, n)] = top
        s = q if d == 0 else partner(q, d, n_vcol)
        g = s * pieces + p
        dest = g // per_chunk
        place = g - dest * per_chunk
        to = {"field": dest}
        c = pltpu.make_async_remote_copy(
            src_ref=code.at[d, p], dst_ref=got.at[f, place],
            send_sem=part_send.at[d, p], recv_sem=part_recv.at[f, place],
            device_id=to, device_id_type=MESH,
        )
        t = pltpu.make_async_remote_copy(
            src_ref=tops.at[d, p], dst_ref=got_tops.at[f, place],
            send_sem=top_send.at[d, p], recv_sem=top_recv.at[f, place],
            device_id=to, device_id_type=MESH,
        )

        @pl.when(dest != f)
        def _():
            t.start()
            c.start()

        @pl.when(dest == f)
        def _():
            mine_sum[place] = part[d, p]

        part_sends.append((dest, c, t))

    def forward(p):
        first = pl.ds(p * width, width // 2)
        second = pl.ds(p * width + width // 2, width - width // 2)
        row_copy[1, p].wait_recv()
        a = send(rows.at[1, first], rows.at[3, first],
                 row_send.at[3, p], row_recv.at[3, p], {"vcol": partner(q, 2, 4)})
        row_copy[2, p].wait_recv()
        b = send(rows.at[2, second], rows.at[3, second],
                 row_send.at[0, p], row_recv.at[0, p], {"vcol": partner(q, 1, 4)})
        row_copy[3, p] = (a, b)
        if p + AHEAD < pieces:
            send_rows(p + AHEAD)

    compute(0, 0)
    for p in range(pieces):
        if relay:
            forward(p)
        for d in range(1, 3 if relay else n_vcol):
            if not relay:
                row_copy[d, p].wait_recv()
            compute(d, p)
        if p + 1 < pieces:
            compute(0, p + 1)
        if relay and p:
            for c in row_copy[3, p - 1]:
                c.wait_recv()
            compute(3, p - 1)
    if relay:
        for c in row_copy[3, pieces - 1]:
            c.wait_recv()
        compute(3, pieces - 1)

    for place in range(per_chunk):
        total = mine_sum[place]
        for d in range(1, n_field):
            src = lax.rem(f + d, n_field)
            for buf, land, gone, came in (
                (code, got, part_send, part_recv), (tops, got_tops, top_send, top_recv),
            ):
                pltpu.make_async_remote_copy(
                    src_ref=buf.at[0, 0], dst_ref=land.at[src, place],
                    send_sem=gone.at[0, 0], recv_sem=came.at[src, place],
                    device_id={"field": src}, device_id_type=MESH,
                ).wait_recv()
            level = (got[src, place].astype(jnp.int32) + HALF).astype(jnp.float32)
            total = total + level * (got_tops[src, place] * (1.0 / LEVELS))
        total = total * scale
        parts = n_vrow * ch
        for k in range(parts):
            out[pl.ds(place * ch * width * parts + k, ch * width, parts), :] = total[:, k * vs : (k + 1) * vs]
    for c in sends:
        c.wait_send()
    for dest, c, t in part_sends:
        @pl.when(dest != f)
        def _():
            c.wait_send()
            t.wait_send()


def on_device(blocks, block_ids, block_counts):
    n_field, n_vrow, n_vcol = (lax.axis_size(a) for a in ("field", "vrow", "vcol"))
    vs, occ, ch, x = blocks.shape
    chunk = n_vcol * vs // n_field
    width = min(vs // MAX_PIECES, chunk)
    pieces = vs // width
    per_chunk = chunk // width
    data = blocks
    slots = jnp.arange(occ, dtype=jnp.int32)
    ids = jnp.where(slots < block_counts[0, 0], block_ids[0, 0], -1)
    meta = jnp.pad(ids[None, :], ((0, 0), (0, 128 - occ)))
    c = ch * vs
    wide = n_vrow * c
    dims = (n_field, n_vrow, n_vcol, pieces, occ, width, per_chunk)
    dma = pltpu.SemaphoreType.DMA
    scale = 1.0 / (n_field * SBLK * BLOCK)
    out = pl.pallas_call(
        functools.partial(kernel, dims, scale),
        out_shape=jax.ShapeDtypeStruct((chunk * ch * n_vrow * ch, vs), jnp.float32),
        in_specs=[pl.BlockSpec(memory_space=pl.ANY), pl.BlockSpec(memory_space=pltpu.VMEM)],
        out_specs=pl.BlockSpec(memory_space=pltpu.VMEM),
        scratch_shapes=[
            pltpu.VMEM((n_vcol, vs, occ, ch, x), jnp.bfloat16),
            pltpu.VMEM((n_vrow, vs, occ, ch, x), jnp.bfloat16),
            pltpu.VMEM((n_vrow, occ + 1, ch * vs, x), jnp.bfloat16),
            pltpu.VMEM((n_vcol, pieces, ch * width, wide), jnp.float32),
            pltpu.VMEM((n_vcol, pieces, ch * width, wide), jnp.int16),
            pltpu.VMEM((n_vcol, pieces, 1, wide), jnp.float32),
            pltpu.VMEM((n_field, per_chunk, ch * width, wide), jnp.int16),
            pltpu.VMEM((n_field, per_chunk, 1, wide), jnp.float32),
            pltpu.VMEM((per_chunk, ch * width, wide), jnp.float32),
            pltpu.VMEM((n_vcol, 1, 128), jnp.int32),
            pltpu.VMEM((n_vrow, 1, 128), jnp.int32),
            pltpu.SMEM((n_vcol, 1, 128), jnp.int32),
            pltpu.SMEM((n_vrow, 1, 128), jnp.int32),
            dma((1,)),
            dma((2,)),
            dma((n_vcol, pieces)),
            dma((n_vcol, pieces)),
            dma((n_vrow, pieces)),
            dma((n_vrow, pieces)),
            dma((n_vcol,)),
            dma((n_vcol,)),
            dma((n_vrow,)),
            dma((n_vrow,)),
            dma((n_vcol, pieces)),
            dma((n_field, per_chunk)),
            dma((n_vcol, pieces)),
            dma((n_field, per_chunk)),
        ],
        compiler_params=pltpu.CompilerParams(collective_id=0, has_side_effects=True),
    )(data, meta)
    return out.reshape(chunk, ch, n_vrow, 1, ch, vs)


def solution(mesh):
    placed = (
        P(("vrow", "vcol"), "field", None, None),
        P(("vrow", "vcol"), "field", None),
        P(("vrow", "vcol"), "field"),
    )
    return jax.shard_map(
        on_device,
        mesh=mesh,
        in_specs=placed,
        out_specs=P(("vrow", "field"), None, None, "vcol", None, None),
        check_vma=False,
    )
```

```python
import functools

import jax
import jax.numpy as jnp
from jax import lax
from jax.experimental import pallas as pl
from jax.experimental.pallas import tpu as pltpu
from jax.sharding import PartitionSpec as P

SBLK = 12
BLOCK = 256
MAX_PIECES = 4
AHEAD = 2
LEVELS = 65535.0
HALF = 32768
MESH = pl.DeviceIdType.MESH


def partner(q, d, n):
    if n == 4:
        return (q + 1 - 2 * lax.rem(q, 2), lax.rem(q + 2, 4), 3 - q)[d - 1]
    return lax.rem(q + d, n)


def kernel(
    dims, scale, data, ids, counts, out, meta, rows, raw_cols, cols, part, code, tops, got, got_tops, mine_sum, rmeta, cmeta, rids, cids,
    row_local, meta_local,
    row_send, row_recv, col_send, col_recv, rm_send, rm_recv, cm_send, cm_recv,
    part_send, part_recv, top_send, top_recv,
):
    n_field, n_vrow, n_vcol, pieces, occ, width, per_chunk = dims
    f, r, q = lax.axis_index("field"), lax.axis_index("vrow"), lax.axis_index("vcol")
    relay = n_vcol == 4

    barrier = pltpu.get_barrier_semaphore()
    for d in range(1, n_vcol):
        pl.semaphore_signal(barrier, inc=1, device_id={"vcol": partner(q, d, n_vcol)}, device_id_type=MESH)
    for d in range(1, n_vrow):
        pl.semaphore_signal(barrier, inc=1, device_id={"vrow": lax.rem(r + d, n_vrow)}, device_id_type=MESH)
    for d in range(1, n_field):
        pl.semaphore_signal(barrier, inc=1, device_id={"field": lax.rem(f + d, n_field)}, device_id_type=MESH)

    meta[...] = jnp.full_like(meta, -1)
    slots = lax.broadcasted_iota(jnp.int32, (1, occ), 1)
    meta[:, 0:occ] = jnp.where(slots < counts[...], ids[0], -1)
    own = pltpu.make_async_copy(data, rows.at[0], row_local.at[0])
    own.start()
    for v in range(n_vrow):
        cols[v, occ] = jnp.zeros_like(cols[v, occ])

    pl.semaphore_wait(barrier, n_vcol + n_vrow + n_field - 3)

    own_r = pltpu.make_async_copy(meta, rids.at[0], meta_local.at[0])
    own_r.start()
    own_c = pltpu.make_async_copy(meta, cids.at[0], meta_local.at[1])
    own_c.start()

    def span(p):
        return pl.ds(p * width, width)

    sends = []

    def send(src, dst, s, w, where):
        c = pltpu.make_async_remote_copy(
            src_ref=src, dst_ref=dst, send_sem=s, recv_sem=w, device_id=where, device_id_type=MESH
        )
        c.start()
        sends.append(c)
        return c

    row_meta, col_meta, row_copy, col_copy = {}, {}, {}, {}

    def send_rows(p):
        for d in range(1, 3 if relay else n_vcol):
            to = {"vcol": partner(q, d, n_vcol)}
            row_copy[d, p] = send(data.at[span(p)], rows.at[d, span(p)], row_send.at[d, p], row_recv.at[d, p], to)

    for d in range(1, n_vrow):
        to = {"vrow": lax.rem(r + d, n_vrow)}
        col_meta[d] = send(meta, cmeta.at[d], cm_send.at[d], cm_recv.at[d], to)
    for d in range(1, n_vcol):
        to = {"vcol": partner(q, d, n_vcol)}
        row_meta[d] = send(meta, rmeta.at[d], rm_send.at[d], rm_recv.at[d], to)
    for p in range(pieces):
        for d in range(1, n_vrow):
            to = {"vrow": lax.rem(r + d, n_vrow)}
            col_copy[d, p] = send(
                data.at[span(p)],
                raw_cols.at[d, span(p)],
                col_send.at[d, p], col_recv.at[d, p], to,
            )
        if p < (AHEAD if relay else pieces):
            send_rows(p)

    own.wait()
    own_r.wait()
    own_c.wait()
    for d in range(1, n_vrow):
        col_meta[d].wait_recv()
        c = pltpu.make_async_copy(cmeta.at[d], cids.at[d], meta_local.at[1])
        c.start()
        c.wait()
    for d in range(1, n_vrow):
        for p in range(pieces):
            col_copy[d, p].wait_recv()
    ch, vs = rows.shape[3], rows.shape[1]
    n = ch * vs
    to_row = lax.broadcasted_iota(jnp.int32, (n, n), 0)
    from_row = lax.broadcasted_iota(jnp.int32, (n, n), 1)
    order = jnp.where(from_row == lax.rem(to_row, vs) * ch + to_row // vs, 1.0, 0.0).astype(jnp.bfloat16)
    for v in range(n_vrow):
        for o in range(occ):
            block = (raw_cols[v, :, o] if v else rows[0, :, o]).reshape(n, rows.shape[-1])
            turned = jnp.dot(order, block, preferred_element_type=jnp.float32)
            cols[v, o] = turned.astype(jnp.bfloat16)

    match = {}
    part_sends = []

    def matches(d):
        if d:
            row_meta[d].wait_recv()
            c = pltpu.make_async_copy(rmeta.at[d], rids.at[d], meta_local.at[0])
            c.start()
            c.wait()
        theirs = [[cids[v, 0, o] for o in range(occ)] for v in range(n_vrow)]
        found = []
        for o in range(occ):
            mine = rids[d, 0, o]
            for v in range(n_vrow):
                m = jnp.int32(occ)
                for k in range(occ):
                    m = jnp.where((mine >= 0) & (mine == theirs[v][k]), jnp.int32(k), m)
                found.append(m)
        return found

    def compute(d, p):
        if d not in match:
            match[d] = matches(d)
        for v in range(n_vrow):
            acc = None
            for o in range(occ):
                lhs = rows[d, p * width : (p + 1) * width, o].reshape(ch * width, rows.shape[-1])
                rhs = cols[v, match[d][o * n_vrow + v]]
                t = lax.dot_general(lhs, rhs, (((1,), (1,)), ((), ())), preferred_element_type=jnp.float32)
                acc = t if acc is None else acc + t
            n = acc.shape[1]
            at = pl.multiple_of(lax.rem(r + v, n_vrow) * n, n)
            part[d, p, :, pl.ds(at, n)] = acc
            top = jnp.max(acc, axis=0, keepdims=True)
            inverse = jnp.where(top > 0, 1.0 / top, 0.0)
            level = ((acc * inverse) * LEVELS + 0.5).astype(jnp.int32) - HALF
            code[d, p, :, pl.ds(at, n)] = level.astype(jnp.int16)
            tops[d, p, :, pl.ds(at, n)] = top
        s = q if d == 0 else partner(q, d, n_vcol)
        g = s * pieces + p
        dest = g // per_chunk
        place = g - dest * per_chunk
        to = {"field": dest}
        c = pltpu.make_async_remote_copy(
            src_ref=code.at[d, p], dst_ref=got.at[f, place],
            send_sem=part_send.at[d, p], recv_sem=part_recv.at[f, place],
            device_id=to, device_id_type=MESH,
        )
        t = pltpu.make_async_remote_copy(
            src_ref=tops.at[d, p], dst_ref=got_tops.at[f, place],
            send_sem=top_send.at[d, p], recv_sem=top_recv.at[f, place],
            device_id=to, device_id_type=MESH,
        )

        @pl.when(dest != f)
        def _():
            t.start()
            c.start()

        @pl.when(dest == f)
        def _():
            mine_sum[place] = part[d, p]

        part_sends.append((dest, c, t))

    def forward(p):
        first = pl.ds(p * width, width // 2)
        second = pl.ds(p * width + width // 2, width - width // 2)
        row_copy[1, p].wait_recv()
        a = send(rows.at[1, first], rows.at[3, first],
                 row_send.at[3, p], row_recv.at[3, p], {"vcol": partner(q, 2, 4)})
        row_copy[2, p].wait_recv()
        b = send(rows.at[2, second], rows.at[3, second],
                 row_send.at[0, p], row_recv.at[0, p], {"vcol": partner(q, 1, 4)})
        row_copy[3, p] = (a, b)
        if p + AHEAD < pieces:
            send_rows(p + AHEAD)

    compute(0, 0)
    for p in range(pieces):
        if relay:
            forward(p)
        for d in range(1, 3 if relay else n_vcol):
            if not relay:
                row_copy[d, p].wait_recv()
            compute(d, p)
        if p + 1 < pieces:
            compute(0, p + 1)
        if relay and p:
            for c in row_copy[3, p - 1]:
                c.wait_recv()
            compute(3, p - 1)
    if relay:
        for c in row_copy[3, pieces - 1]:
            c.wait_recv()
        compute(3, pieces - 1)

    for place in range(per_chunk):
        total = mine_sum[place]
        for d in range(1, n_field):
            src = lax.rem(f + d, n_field)
            for buf, land, gone, came in (
                (code, got, part_send, part_recv), (tops, got_tops, top_send, top_recv),
            ):
                pltpu.make_async_remote_copy(
                    src_ref=buf.at[0, 0], dst_ref=land.at[src, place],
                    send_sem=gone.at[0, 0], recv_sem=came.at[src, place],
                    device_id={"field": src}, device_id_type=MESH,
                ).wait_recv()
            level = (got[src, place].astype(jnp.int32) + HALF).astype(jnp.float32)
            total = total + level * (got_tops[src, place] * (1.0 / LEVELS))
        parts = n_vrow * ch
        for k in range(parts):
            out[pl.ds(place * ch * width * parts + k, ch * width, parts), :] = total[:, k * vs : (k + 1) * vs]
    for c in sends:
        c.wait_send()
    for dest, c, t in part_sends:
        @pl.when(dest != f)
        def _():
            c.wait_send()
            t.wait_send()


def on_device(blocks, block_ids, block_counts):
    n_field, n_vrow, n_vcol = (lax.axis_size(a) for a in ("field", "vrow", "vcol"))
    vs, occ, ch, x = blocks.shape
    chunk = n_vcol * vs // n_field
    width = min(vs // MAX_PIECES, chunk)
    pieces = vs // width
    per_chunk = chunk // width
    data = blocks
    c = ch * vs
    wide = n_vrow * c
    dims = (n_field, n_vrow, n_vcol, pieces, occ, width, per_chunk)
    dma = pltpu.SemaphoreType.DMA
    scale = 1.0 / (n_field * SBLK * BLOCK)
    out = pl.pallas_call(
        functools.partial(kernel, dims, scale),
        out_shape=jax.ShapeDtypeStruct((chunk * ch * n_vrow * ch, vs), jnp.float32),
        in_specs=[pl.BlockSpec(memory_space=pl.ANY)] + [pl.BlockSpec(memory_space=pltpu.VMEM)] * 2,
        out_specs=pl.BlockSpec(memory_space=pltpu.VMEM),
        scratch_shapes=[
            pltpu.VMEM((1, 128), jnp.int32),
            pltpu.VMEM((n_vcol, vs, occ, ch, x), jnp.bfloat16),
            pltpu.VMEM((n_vrow, vs, occ, ch, x), jnp.bfloat16),
            pltpu.VMEM((n_vrow, occ + 1, ch * vs, x), jnp.bfloat16),
            pltpu.VMEM((n_vcol, pieces, ch * width, wide), jnp.float32),
            pltpu.VMEM((n_vcol, pieces, ch * width, wide), jnp.int16),
            pltpu.VMEM((n_vcol, pieces, 1, wide), jnp.float32),
            pltpu.VMEM((n_field, per_chunk, ch * width, wide), jnp.int16),
            pltpu.VMEM((n_field, per_chunk, 1, wide), jnp.float32),
            pltpu.VMEM((per_chunk, ch * width, wide), jnp.float32),
            pltpu.VMEM((n_vcol, 1, 128), jnp.int32),
            pltpu.VMEM((n_vrow, 1, 128), jnp.int32),
            pltpu.SMEM((n_vcol, 1, 128), jnp.int32),
            pltpu.SMEM((n_vrow, 1, 128), jnp.int32),
            dma((1,)),
            dma((2,)),
            dma((n_vcol, pieces)),
            dma((n_vcol, pieces)),
            dma((n_vrow, pieces)),
            dma((n_vrow, pieces)),
            dma((n_vcol,)),
            dma((n_vcol,)),
            dma((n_vrow,)),
            dma((n_vrow,)),
            dma((n_vcol, pieces)),
            dma((n_field, per_chunk)),
            dma((n_vcol, pieces)),
            dma((n_field, per_chunk)),
        ],
        compiler_params=pltpu.CompilerParams(collective_id=0, has_side_effects=True),
    )(data, block_ids, block_counts)
    return (out * scale).reshape(chunk, ch, n_vrow, 1, ch, vs)


def solution(mesh):
    placed = (
        P(("vrow", "vcol"), "field", None, None),
        P(("vrow", "vcol"), "field", None),
        P(("vrow", "vcol"), "field"),
    )
    return jax.shard_map(
        on_device,
        mesh=mesh,
        in_specs=placed,
        out_specs=P(("vrow", "field"), None, None, "vcol", None, None),
        check_vma=False,
    )
```
